256 devices in a mesh: wide: 32 (over x_lo, z, core), rows: 8 (over y, x_hi).
Axes of the slice: x: 4 (x_hi: 2, x_lo: 2; x = x_hi * 2 + x_lo), y: 4, z: 8, core: 2. Of those that a mesh axis runs over, the one named last changes fastest.
Arguments:
- matrix: float32 [8192, 16384], P('rows', 'wide'), may hold values from -600 to 600, as said below
- pairing: int32 [2, 512], replicated, may hold values from 0 to 511, each once within a row
Outputs:
- rotated: float32 [8192, 16384], P('rows', 'wide')
The draws below stay inside these ranges and needn't reach their ends.
Inputs may be any that keep to these rules, and one draw needn't show every extreme that they name: `matrix`: finite entries.
All inputs are finite; a program needn't handle non-finite values.
Results may differ from the reference program's by a relative error of at most 0.0001.
Values sent between devices are 32-bit elements; how exact they have to be, the bound alone decides.
A program may use at most 64 MiB of HBM per device.

```python
import math
import jax
import jax.numpy as jnp
from jax import lax

BLOCK = 256
ROUNDS = 2
NS_STEPS = 3
ROWS = 8192
NCOL = 16384
N_WIDE = 32


def draw_matrix(key, part):
    k_noise, k_scale, k_common, k_mix, k_ramp, k_peak = jax.random.split(jax.random.fold_in(key, 11), 6)
    blocks = NCOL // (2 * BLOCK)
    pair_of = (jnp.arange(NCOL) // (2 * BLOCK)).astype(jnp.int32)
    base_draw = jax.random.uniform(k_ramp, (blocks,), jnp.float32, 0.0, 1.0)
    common = jnp.clip(jax.random.normal(k_common, (ROWS,), jnp.float32), -6.0, 6.0)
    mixing = jnp.clip(jax.random.normal(k_mix, (NCOL,), jnp.float32), -6.0, 6.0)
    center = jax.random.randint(k_peak, (), 0, blocks // 2 - 1).astype(jnp.int32)
    noise = jnp.clip(jax.random.normal(k_noise, (ROWS, NCOL), jnp.float32), -6.0, 6.0)
    scales = jnp.exp(jax.random.uniform(k_scale, (NCOL,), jnp.float32, 0.0, math.log(10.0)))
    base = 0.05 + 0.1 * base_draw
    peak = 0.3
    at_peak = (pair_of == center) | (pair_of == center + 1)
    strength = jnp.where(at_peak, jnp.float32(peak), base[pair_of])
    return (noise + common[:, None] * (strength * mixing)[None, :]) * scales[None, :]


def setup_inputs(seed: int = 0) -> dict:
    arg_keys = jax.random.split(jax.random.key(seed), 3)
    matrix = draw_matrix(jax.random.fold_in(arg_keys[2], 71), 0)
    pairing = jax.vmap(lambda own: jax.random.permutation(own, 2 * BLOCK))(jax.random.split(arg_keys[1], ROUNDS)).reshape((ROUNDS, 2 * BLOCK)).astype(jnp.int32)
    return dict(matrix=matrix, pairing=pairing)


EPSILON = 1e-06
HIGH = lax.Precision.HIGHEST

def generator(coupling, largest):
    pairs, half_cols = (coupling.shape[0], coupling.shape[1])
    identity = jnp.broadcast_to(jnp.eye(half_cols, dtype=jnp.float32), (pairs, half_cols, half_cols))
    top = jnp.concatenate([identity, coupling], axis=2)
    bottom = jnp.concatenate([-jnp.transpose(coupling, (0, 2, 1)), identity], axis=2)
    return jnp.concatenate([top, bottom], axis=1) * lax.rsqrt(1.0 + largest)

def reference(matrix, pairing):
    width = matrix.shape[1] // N_WIDE
    half_cols = width // 2
    current = jnp.transpose(matrix.reshape(ROWS, N_WIDE, width), (1, 0, 2))
    for round_index in range(ROUNDS):
        columns = jnp.take(current, pairing[round_index].astype(jnp.int32), axis=2)
        gram = jnp.einsum('pra,prb->pab', columns, columns, precision=HIGH)
        norms = jnp.diagonal(gram, axis1=1, axis2=2)
        inverse = lax.rsqrt(norms + EPSILON)
        coupling = gram[:, :half_cols, half_cols:] * inverse[:, :half_cols, None] * inverse[:, None, half_cols:]
        largest = jnp.max(lax.optimization_barrier(jnp.sum(coupling * coupling, axis=(1, 2))))
        rotation = generator(coupling, largest)
        for sweep in range(NS_STEPS):
            square = jnp.einsum('pca,pcb->pab', rotation, rotation, precision=HIGH)
            rotation = 1.5 * rotation - 0.5 * jnp.einsum('pac,pcb->pab', rotation, square, precision=HIGH)
        product = jnp.einsum('pra,pab->prb', columns, rotation, precision=HIGH)
        kept = product[:, :, :half_cols]
        moved = jnp.roll(product[:, :, half_cols:], 1, axis=0)
        current = jnp.concatenate([kept, moved], axis=2)
    return jnp.transpose(current, (1, 0, 2)).reshape(ROWS, N_WIDE * width)
```

```python
import functools

import jax
import jax.numpy as jnp
from jax import lax
from jax.experimental import pallas as pl
from jax.experimental.pallas import tpu as pltpu
from jax.sharding import PartitionSpec as P

EPSILON = 1e-06
F32 = jnp.float32
BF16 = jnp.bfloat16
CHUNKS = 4
MESH = pl.DeviceIdType.MESH


def split(value):
    high = value.astype(BF16)
    low = (value - high.astype(F32)).astype(BF16)
    return high, low


def dot(left, right, dims=((1,), (0,))):
    return lax.dot_general(left, right, (dims, ((), ())), preferred_element_type=F32)


def mul(left, right, dims=((1,), (0,))):
    return (
        dot(left[0], right[0], dims)
        + dot(left[0], right[1], dims)
        + dot(left[1], right[0], dims)
    )


def total(value):
    return jnp.sum(jnp.sum(value, axis=0, keepdims=True), axis=1, keepdims=True)


def kernel(
    n_wide, n_rows, n_rounds,
    x_ref, pairing_ref, out_ref,
    gram_out, gram_in, slice_out, slices, peak_out, peaks,
    current, cols_h, cols_l, u_h, u_l, v_h, v_l, moved,
    gram_acc, norm_acc,
    gram_send, gram_recv, slice_send, slice_recv, peak_send, peak_recv, move_send, move_recv,
):
    rows, width = x_ref.shape
    half = width // 2
    part = half // n_rows
    step = rows // CHUNKS
    me_w = lax.axis_index("wide")
    me_r = lax.axis_index("rows")

    barrier = pltpu.get_barrier_semaphore()
    for k in range(1, n_rows):
        pl.semaphore_signal(
            barrier, inc=1, device_id={"rows": lax.rem(me_r + k, n_rows)}, device_id_type=MESH
        )

    @pl.loop(1, n_wide)
    def _(k):
        pl.semaphore_signal(
            barrier, inc=1, device_id={"wide": lax.rem(me_w + k, n_wide)}, device_id_type=MESH
        )

    eye = (
        lax.broadcasted_iota(jnp.int32, (half, half), 0)
        == lax.broadcasted_iota(jnp.int32, (half, half), 1)
    ).astype(F32)

    for t in range(n_rounds):
        last = t == n_rounds - 1
        order = (
            lax.broadcasted_iota(jnp.int32, (width, width), 0) == pairing_ref[t : t + 1, :]
        ).astype(BF16)
        gram_acc[...] = jnp.zeros_like(gram_acc)
        norm_acc[...] = jnp.zeros_like(norm_acc)
        for chunk in range(CHUNKS):
            at = pl.ds(chunk * step, step)
            if t == 0:
                block = x_ref[at, :]
            else:
                pltpu.make_async_copy(
                    moved.at[t - 1, chunk], moved.at[t - 1, chunk], move_recv.at[t - 1, chunk]
                ).wait()
                block = jnp.concatenate([current[at, :], moved[t - 1, chunk]], axis=1)
            high, low = split(block)
            high = dot(high, order)
            low = dot(low, order)
            value = high + low
            norm_acc[...] += jnp.sum(value * value, axis=0, keepdims=True)
            high, low = high.astype(BF16), low.astype(BF16)
            cols_h[at, :] = high
            cols_l[at, :] = low
            gram_acc[...] += mul(
                (high[:, :half], low[:, :half]), (high[:, half:], low[:, half:]), ((0,), (0,))
            )

        for k in range(n_rows):
            gram_out[t, k, 0:part, :] = gram_acc[k * part : (k + 1) * part, :]
            gram_out[t, k, part : part + 1, :] = norm_acc[:, :half]
            gram_out[t, k, part + 1 : part + 2, :] = norm_acc[:, half:]
        if t == 0:
            pl.semaphore_wait(barrier, n_rows - 1 + n_wide - 1)
        for k in range(1, n_rows):
            peer = lax.rem(me_r + k, n_rows)
            pltpu.make_async_remote_copy(
                src_ref=gram_out.at[t, peer],
                dst_ref=gram_in.at[t, me_r],
                send_sem=gram_send.at[t],
                recv_sem=gram_recv.at[t],
                device_id={"rows": peer},
                device_id_type=MESH,
            ).start()
        gram_in[t, me_r] = gram_out[t, me_r]
        seven = pl.ds(0, n_rows - 1)
        pltpu.make_async_copy(gram_in.at[t, seven], gram_in.at[t, seven], gram_recv.at[t]).wait()
        summed = gram_in[t, 0]
        for k in range(1, n_rows):
            summed = summed + gram_in[t, k]
        inverse_a = lax.rsqrt(summed[part : part + 1, :] + EPSILON)
        inverse_b = lax.rsqrt(summed[part + 1 : part + 2, :] + EPSILON)
        mine = (
            lax.broadcasted_iota(jnp.int32, (part, half), 0) + me_r * part
            == lax.broadcasted_iota(jnp.int32, (part, half), 1)
        )
        column = jnp.sum(jnp.where(mine, inverse_a, 0.0), axis=1, keepdims=True)
        share = summed[0:part, :] * column * inverse_b
        slice_out[t] = share
        slices[t, me_r] = share
        for k in range(1, n_rows):
            peer = lax.rem(me_r + k, n_rows)
            pltpu.make_async_remote_copy(
                src_ref=slice_out.at[t],
                dst_ref=slices.at[t, me_r],
                send_sem=slice_send.at[t],
                recv_sem=slice_recv.at[t],
                device_id={"rows": peer},
                device_id_type=MESH,
            ).start()
        pltpu.make_async_copy(slices.at[t, seven], slices.at[t, seven], slice_recv.at[t]).wait()
        coupling = slices[t].reshape(half, half)
        own = total(coupling * coupling)
        peak_out[t] = jnp.broadcast_to(own, peak_out.shape[1:])
        peaks[t, me_w] = jnp.broadcast_to(own, peak_out.shape[1:])

        @pl.loop(1, n_wide)
        def _(k):
            pltpu.make_async_remote_copy(
                src_ref=peak_out.at[t],
                dst_ref=peaks.at[t, me_w],
                send_sem=peak_send.at[t],
                recv_sem=peak_recv.at[t],
                device_id={"wide": lax.rem(me_w + k, n_wide)},
                device_id_type=MESH,
            ).start()

        flipped = coupling.T
        c = split(coupling)
        ct = split(flipped)
        for chunk in range(CHUNKS):
            at = pl.ds(chunk * step, step)
            high, low = cols_h[at, :], cols_l[at, :]
            a = (high[:, :half], low[:, :half])
            b = (high[:, half:], low[:, half:])
            u = a[0].astype(F32) + a[1].astype(F32) - mul(b, ct)
            v = b[0].astype(F32) + b[1].astype(F32) + mul(a, c)
            u_h[at, :], u_l[at, :] = split(u)
            v_h[at, :], v_l[at, :] = split(v)
        scale = 1.0 / (1.0 + own)
        powers = []
        for left, right in ((c, ct), (ct, c)):
            first = (eye + mul(left, right)) * scale
            pieces = split(first)
            second = mul(pieces, pieces)
            third = mul(split(second), pieces)
            powers.append((first, second, third))

        others = pl.ds(0, n_wide - 1)
        pltpu.make_async_copy(peaks.at[t, others], peaks.at[t, others], peak_recv.at[t]).wait()
        largest = jnp.max(peaks[t], axis=0)[0:1, 0:1]
        root = lax.rsqrt(1.0 + largest)
        ratio = (1.0 + own) / (1.0 + largest)
        factors = []
        for first, second, third in powers:
            n1 = (2.25 * ratio) * first - (1.5 * ratio * ratio) * second
            n1 = n1 + (0.25 * ratio * ratio * ratio) * third
            t1 = split(1.5 * eye - 0.5 * n1)
            q1 = root * (1.5 * eye - (0.5 * ratio) * first)
            n2 = mul(split(mul(split(n1), t1)), t1)
            q2 = mul(split(q1), t1)
            t2 = split(1.5 * eye - 0.5 * n2)
            factors.append(split(mul(split(q2), t2)))

        for chunk in range(CHUNKS):
            at = pl.ds(chunk * step, step)
            moved[n_rounds + t, chunk] = mul((v_h[at, :], v_l[at, :]), factors[1])
            pltpu.make_async_remote_copy(
                src_ref=moved.at[n_rounds + t, chunk],
                dst_ref=moved.at[t, chunk],
                send_sem=move_send.at[t, chunk],
                recv_sem=move_recv.at[t, chunk],
                device_id={"wide": lax.rem(me_w + 1, n_wide)},
                device_id_type=MESH,
            ).start()
        for chunk in range(CHUNKS):
            at = pl.ds(chunk * step, step)
            kept = mul((u_h[at, :], u_l[at, :]), factors[0])
            if last:
                out_ref[at, 0:half] = kept
            else:
                current[at, :] = kept
        pltpu.make_async_copy(gram_out.at[t, seven], gram_out.at[t, seven], gram_send.at[t]).wait()
        pltpu.make_async_copy(slices.at[t, seven], slices.at[t, seven], slice_send.at[t]).wait()
        pltpu.make_async_copy(peaks.at[t, others], peaks.at[t, others], peak_send.at[t]).wait()
        if last:
            for chunk in range(CHUNKS):
                at = pl.ds(chunk * step, step)
                pltpu.make_async_copy(
                    moved.at[t, chunk], moved.at[t, chunk], move_recv.at[t, chunk]
                ).wait()
                out_ref[at, half:width] = moved[t, chunk]
    for t in range(n_rounds):
        for chunk in range(CHUNKS):
            sent = moved.at[n_rounds + t, chunk]
            pltpu.make_async_copy(sent, sent, move_send.at[t, chunk]).wait()


def solution(mesh):
    n_wide, n_rows = mesh.shape["wide"], mesh.shape["rows"]

    def shards(matrix, pairing):
        rows, width = matrix.shape
        half = width // 2
        part = half // n_rows
        n_rounds = pairing.shape[0]
        step = rows // CHUNKS
        vmem = pl.BlockSpec(memory_space=pltpu.VMEM)
        dma = pltpu.SemaphoreType.DMA
        return pl.pallas_call(
            functools.partial(kernel, n_wide, n_rows, n_rounds),
            out_shape=jax.ShapeDtypeStruct(matrix.shape, F32),
            in_specs=[vmem, vmem],
            out_specs=vmem,
            scratch_shapes=[
                pltpu.VMEM((n_rounds, n_rows, part + 8, half), F32),
                pltpu.VMEM((n_rounds, n_rows, part + 8, half), F32),
                pltpu.VMEM((n_rounds, part, half), F32),
                pltpu.VMEM((n_rounds, n_rows, part, half), F32),
                pltpu.VMEM((n_rounds, 8, 128), F32),
                pltpu.VMEM((n_rounds, n_wide, 8, 128), F32),
                pltpu.VMEM((rows, half), F32),
                pltpu.VMEM((rows, width), BF16),
                pltpu.VMEM((rows, width), BF16),
                pltpu.VMEM((rows, half), BF16),
                pltpu.VMEM((rows, half), BF16),
                pltpu.VMEM((rows, half), BF16),
                pltpu.VMEM((rows, half), BF16),
                pltpu.VMEM((2 * n_rounds, CHUNKS, step, half), F32),
                pltpu.VMEM((half, half), F32),
                pltpu.VMEM((1, width), F32),
                dma((n_rounds,)), dma((n_rounds,)), dma((n_rounds,)), dma((n_rounds,)),
                dma((n_rounds,)), dma((n_rounds,)), dma((n_rounds, CHUNKS)), dma((n_rounds, CHUNKS)),
            ],
            compiler_params=pltpu.CompilerParams(
                collective_id=0, has_side_effects=True, vmem_limit_bytes=48 * 1024 * 1024
            ),
        )(matrix, pairing)

    return jax.shard_map(
        shards, mesh=mesh, in_specs=(P("rows", "wide"), P()), out_specs=P("rows", "wide"),
        check_vma=False,
    )
```

```python
import functools

import jax
import jax.numpy as jnp
from jax import lax
from jax.experimental import pallas as pl
from jax.experimental.pallas import tpu as pltpu
from jax.sharding import PartitionSpec as P

EPSILON = 1e-06
F32 = jnp.float32
BF16 = jnp.bfloat16
CHUNKS = 4
RAW = ((0, 256), (256, 192))
PIECES = ((448, 128), (576, 192), (768, 256))
EARLY = 2
RELAY = ((0, 256), (256, 192))
MESH = pl.DeviceIdType.MESH


def split(value):
    high = value.astype(BF16)
    low = (value - high.astype(F32)).astype(BF16)
    return high, low


def dot(left, right, dims=((1,), (0,))):
    return lax.dot_general(left, right, (dims, ((), ())), preferred_element_type=F32)


def mul(left, right, dims=((1,), (0,))):
    return (
        dot(left[0], right[0], dims)
        + dot(left[0], right[1], dims)
        + dot(left[1], right[0], dims)
    )


def total(value):
    return jnp.sum(jnp.sum(value, axis=0, keepdims=True), axis=1, keepdims=True)


def ring(distance, size):
    return min(distance, size - distance)


def row_peers(me_r, n_rows):
    n_y = n_rows // 2
    y, x = me_r // 2, me_r % 2
    offsets = [(dy, dx) for dy in range(n_y) for dx in range(2) if dy or dx]
    offsets.sort(key=lambda o: -(ring(o[0], n_y) + 2 * o[1]))
    return [((y + dy) % n_y) * 2 + (x + dx) % 2 for dy, dx in offsets]


def column_peers(me_w, n_wide):
    n_z = n_wide // 4
    x, z, core = me_w // (2 * n_z), (me_w // 2) % n_z, me_w % 2
    offsets = [(dz, dc) for dz in range(n_z) for dc in range(2) if dz or dc]
    offsets.sort(key=lambda o: -(ring(o[0], n_z) + 0.1 * o[1]))
    return [x * (2 * n_z) + ((z + dz) % n_z) * 2 + (core + dc) % 2 for dz, dc in offsets]


def wait(ref, sem):
    pltpu.make_async_copy(ref, ref, sem).wait()


def kernel(
    n_wide, n_rows, n_rounds,
    x_hbm, pairing_hbm, out_ref,
    x_ref, pairing_ref,
    gram_out, gram_in, part_out, parts, slice_out, slices, peak_out, peaks,
    raw_out, raw_in, v_out, v_in, behinds, crosses, cross, pass_in,
    cols_h, cols_l, u_h, u_l, v_h, v_l, gram_acc, norm_acc,
    x_sem, pairing_sem,
    gram_send, gram_recv, part_send, part_recv, slice_send, slice_recv, peak_send, peak_recv,
    raw_send, raw_recv, v_send, v_recv, relay_send, relay_recv, pass_send, pass_recv,
    c_send, c_recv, d_send, d_recv,
):
    rows, width = x_ref.shape
    half = width // 2
    part = half // n_rows
    step = rows // CHUNKS
    me_w = lax.axis_index("wide")
    me_r = lax.axis_index("rows")
    following = {"wide": lax.rem(me_w + 1, n_wide)}
    column = n_wide // 2
    first_z = lax.rem(me_w, column) == 0
    last_z = lax.rem(me_w, column) == column - 1
    next_z = {"wide": (me_w // column) * column + lax.rem(me_w + 1, column)}
    partner = {"wide": lax.rem(me_w + column, n_wide)}
    me_x, me_c = me_w // column, lax.rem(me_w, column)
    along_rows = [{"rows": peer} for peer in row_peers(me_r, n_rows)]
    along_column = [{"wide": peer} for peer in column_peers(me_w, n_wide)]

    def rows_of(pair):
        far = [{"wide": pair, "rows": device["rows"]} for device in along_rows]
        return far + [{"wide": pair, "rows": me_r}]


    def send(source, target, send_sem, recv_sem, device):
        pltpu.make_async_remote_copy(
            src_ref=source, dst_ref=target, send_sem=send_sem, recv_sem=recv_sem,
            device_id=device, device_id_type=MESH,
        ).start()

    pltpu.make_async_copy(pairing_hbm, pairing_ref, pairing_sem).start()
    for chunk in range(CHUNKS):
        at = pl.ds(chunk * step, step)
        pltpu.make_async_copy(x_hbm.at[at], x_ref.at[at], x_sem.at[chunk]).start()
    barrier = pltpu.get_barrier_semaphore()

    def greet(devices):
        for device in devices:
            pl.semaphore_signal(barrier, inc=1, device_id=device, device_id_type=MESH)

    known = along_rows + along_column + rows_of(partner["wide"])
    greet(known)

    @pl.when(last_z)
    def _():
        greet([following])

    @pl.when(first_z)
    def _():
        greet([{"wide": lax.rem(me_w + n_wide - 1, n_wide)}])


    eye = (
        lax.broadcasted_iota(jnp.int32, (half, half), 0)
        == lax.broadcasted_iota(jnp.int32, (half, half), 1)
    ).astype(F32)
    mine = (
        lax.broadcasted_iota(jnp.int32, (part, half), 0) + me_r * part
        == lax.broadcasted_iota(jnp.int32, (part, half), 1)
    )
    pltpu.make_async_copy(pairing_hbm, pairing_ref, pairing_sem).wait()
    factors = None
    raw_rows = sum(size for _, size in RAW)

    def send_raw(t, k):
        at = pl.ds(*RAW[k])
        send(raw_out.at[t, at], raw_in.at[t, at], raw_send.at[t, k], raw_recv.at[t, k], next_z)

    def finished(t, chunk):
        at = pl.ds(chunk * step, step)
        kept = mul((u_h[at, :], u_l[at, :]), factors[0])
        for k, (start, size) in enumerate(PIECES):
            if chunk * step <= start < (chunk + 1) * step:
                rows_at = pl.ds(start, size)
                wait(v_in.at[t, rows_at], v_recv.at[t, k])
                v_h[rows_at, :], v_l[rows_at, :] = split(v_in[t, rows_at, :])
        for k, (start, size) in enumerate(RELAY):
            if chunk * step <= start < (chunk + 1) * step:
                rows_at = pl.ds(start, size)

                @pl.when(first_z)
                def _():
                    wait(v_in.at[t, rows_at], relay_recv.at[t, k])
                    v_h[rows_at, :], v_l[rows_at, :] = split(v_in[t, rows_at, :])

        return jnp.concatenate([kept, mul((v_h[at, :], v_l[at, :]), factors[1])], axis=1)

    for t in range(n_rounds):
        order = (
            lax.broadcasted_iota(jnp.int32, (width, width), 0) == pairing_ref[t : t + 1, :]
        ).astype(BF16)
        gram_acc[...] = jnp.zeros_like(gram_acc)
        norm_acc[...] = jnp.zeros_like(norm_acc)
        for chunk in range(CHUNKS):
            at = pl.ds(chunk * step, step)
            if t == 0:
                pltpu.make_async_copy(x_hbm.at[at], x_ref.at[at], x_sem.at[chunk]).wait()
                block = x_ref[at, :]
            else:
                block = finished(t - 1, chunk)
            high, low = split(block)
            high = dot(high, order)
            low = dot(low, order)
            value = high + low
            if chunk * step < raw_rows:
                size = min(step, raw_rows - chunk * step)
                raw_out[t, pl.ds(chunk * step, size), :] = value[:size]
                if t > 0:
                    for k, (start, _) in enumerate(RAW):
                        if chunk * step <= start < (chunk + 1) * step:
                            send_raw(t, k)
            norm_acc[...] += jnp.sum(value * value, axis=0, keepdims=True)
            high, low = high.astype(BF16), low.astype(BF16)
            cols_h[at, :] = high
            cols_l[at, :] = low
            gram_acc[...] += mul(
                (high[:, :half], low[:, :half]), (high[:, half:], low[:, half:]), ((0,), (0,))
            )

        for k in range(n_rows):
            gram_out[t, k, 0:part, :] = gram_acc[k * part : (k + 1) * part, :]
            gram_out[t, k, part : part + 1, :] = norm_acc[:, :half]
            gram_out[t, k, part + 1 : part + 2, :] = norm_acc[:, half:]
        if t == 0:
            crossing = jnp.where(jnp.logical_or(first_z, last_z), 1, 0)
            pl.semaphore_wait(barrier, len(known) + crossing)
        for device in along_rows:
            send(
                gram_out.at[t, device["rows"]], gram_in.at[t, me_r],
                gram_send.at[t], gram_recv.at[t], device,
            )
        if t == 0:
            for k in range(len(RAW)):
                send_raw(t, k)
        gram_in[t, me_r] = gram_out[t, me_r]
        seven = pl.ds(0, n_rows - 1)
        all_but_one = pl.ds(0, 2 * n_rows - 1)
        wait(gram_in.at[t, seven], gram_recv.at[t])
        summed = gram_in[t, 0]
        for k in range(1, n_rows):
            summed = summed + gram_in[t, k]
        inverse_a = lax.rsqrt(summed[part : part + 1, :] + EPSILON)
        inverse_b = lax.rsqrt(summed[part + 1 : part + 2, :] + EPSILON)
        scaled = jnp.sum(jnp.where(mine, inverse_a, 0.0), axis=1, keepdims=True)
        share = summed[0:part, :] * scaled * inverse_b

        square = jnp.broadcast_to(total(share * share), (8, 128))
        part_out[t] = square
        place = me_x * n_rows + me_r
        parts[t, place] = square
        across = rows_of(partner["wide"])
        for device in across[:-1] + along_rows + across[-1:]:
            send(part_out.at[t], parts.at[t, place], part_send.at[t], part_recv.at[t], device)
        slice_out[t] = share
        slices[t, me_r] = share
        for device in along_rows:
            send(slice_out.at[t], slices.at[t, me_r], slice_send.at[t], slice_recv.at[t], device)
        wait(parts.at[t, all_but_one], part_recv.at[t])
        peak = parts[t, me_x * n_rows]
        other = parts[t, (1 - me_x) * n_rows]
        for k in range(1, n_rows):
            peak = peak + parts[t, me_x * n_rows + k]
            other = other + parts[t, (1 - me_x) * n_rows + k]
        own = peak[0:1, 0:1]
        peak = jnp.maximum(peak, other)
        peak_out[t] = peak
        peaks[t, me_c] = peak
        for device in along_column:
            send(peak_out.at[t], peaks.at[t, me_c], peak_send.at[t], peak_recv.at[t], device)

        wait(slices.at[t, seven], slice_recv.at[t])
        send(slices.at[t], behinds.at[t], c_send.at[t], c_recv.at[t], following)

        @pl.when(last_z)
        def _():
            send(slices.at[t], crosses.at[t], d_send.at[t], d_recv.at[t], next_z)

        coupling = slices[t].reshape(half, half)
        c = split(coupling)
        for k, (start, size) in enumerate(PIECES):
            at = pl.ds(start, size)
            high, low = cols_h[at, :], cols_l[at, :]
            v = high[:, half:].astype(F32) + low[:, half:].astype(F32)
            v_out[t, at, :] = v + mul((high[:, :half], low[:, :half]), c)

            @pl.when(last_z)
            def _():
                send(v_out.at[t, at], pass_in.at[t, at], pass_send.at[t, k], pass_recv.at[t, k], partner)


        wait(behinds.at[t], c_recv.at[t])
        behind = behinds[t].reshape(half, half)

        @pl.when(first_z)
        def _():
            wait(crosses.at[t], d_recv.at[t])
            cross[...] = crosses[t].reshape(half, half)

        @pl.when(jnp.logical_not(first_z))
        def _():
            cross[...] = behind

        c_cross = split(cross[...])
        for k, (start, size) in enumerate(RAW):
            at = pl.ds(start, size)
            wait(raw_in.at[t, at], raw_recv.at[t, k])
            left, right = raw_in[t, at, 0:half], raw_in[t, at, half:width]
            v = right + mul(split(left), c_cross)
            v_out[t, at, :] = v
            v_h[at, :], v_l[at, :] = split(v)

        ct = split(coupling.T)
        for chunk in range(CHUNKS):
            at = pl.ds(chunk * step, step)
            high, low = cols_h[at, :], cols_l[at, :]
            u = high[:, :half].astype(F32) + low[:, :half].astype(F32)
            u_h[at, :], u_l[at, :] = split(u - mul((high[:, half:], low[:, half:]), ct))

        def powers(left, right, bound):
            first = (eye + mul(left, right)) * (1.0 / (1.0 + bound))
            pieces = split(first)
            second = mul(pieces, pieces)
            return first, second, mul(split(second), pieces)

        kept_powers = powers(c, ct, own)
        c = split(behind)
        ct = split(behind.T)
        own_behind = total(behind * behind)
        moved_powers = powers(ct, c, own_behind)

        others = pl.ds(0, column - 1)
        wait(peaks.at[t, others], peak_recv.at[t])

        @pl.when(first_z)
        def _():
            for k, (start, size) in enumerate(RELAY):
                at = pl.ds(start, size)
                send(v_out.at[t, at], v_in.at[t, at], relay_send.at[t, k], relay_recv.at[t, k], partner)

        @pl.when(jnp.logical_not(last_z))
        def _():
            for k, (start, size) in enumerate(PIECES):
                at = pl.ds(start, size)
                send(v_out.at[t, at], v_in.at[t, at], v_send.at[t, k], v_recv.at[t, k], following)

        def forward(k):
            at = pl.ds(*PIECES[k])
            wait(pass_in.at[t, at], pass_recv.at[t, k])
            send(pass_in.at[t, at], v_in.at[t, at], v_send.at[t, k], v_recv.at[t, k], next_z)

        @pl.when(last_z)
        def _():
            for k in range(EARLY):
                forward(k)

        largest = jnp.max(peaks[t], axis=0)[0:1, 0:1]
        root = lax.rsqrt(1.0 + largest)
        factors = []
        for (first, second, third), bound in ((kept_powers, own), (moved_powers, own_behind)):
            ratio = (1.0 + bound) / (1.0 + largest)
            n1 = (2.25 * ratio) * first - (1.5 * ratio * ratio) * second
            n1 = n1 + (0.25 * ratio * ratio * ratio) * third
            t1 = split(1.5 * eye - 0.5 * n1)
            q1 = root * (1.5 * eye - (0.5 * ratio) * first)
            n2 = mul(split(mul(split(n1), t1)), t1)
            q2 = mul(split(q1), t1)
            t2 = split(1.5 * eye - 0.5 * n2)
            factors.append(split(mul(split(q2), t2)))

        @pl.when(last_z)
        def _():
            for k in range(EARLY, len(PIECES)):
                forward(k)

    for chunk in range(CHUNKS):
        at = pl.ds(chunk * step, step)
        out_ref[at, :] = finished(n_rounds - 1, chunk)

    for t in range(n_rounds):
        wait(gram_out.at[t, seven], gram_send.at[t])
        wait(parts.at[t, all_but_one], part_send.at[t])
        wait(slices.at[t, seven], slice_send.at[t])
        wait(peaks.at[t, others], peak_send.at[t])
        wait(behinds.at[t], c_send.at[t])
        for k, (start, size) in enumerate(RAW):
            wait(raw_out.at[t, pl.ds(start, size)], raw_send.at[t, k])
        for k, (start, size) in enumerate(PIECES):
            wait(v_out.at[t, pl.ds(start, size)], v_send.at[t, k])

        @pl.when(last_z)
        def _():
            wait(crosses.at[t], d_send.at[t])
            for k, (start, size) in enumerate(PIECES):
                wait(v_out.at[t, pl.ds(start, size)], pass_send.at[t, k])

        @pl.when(first_z)
        def _():
            for k, (start, size) in enumerate(RELAY):
                wait(v_out.at[t, pl.ds(start, size)], relay_send.at[t, k])


def solution(mesh):
    n_wide, n_rows = mesh.shape["wide"], mesh.shape["rows"]

    def shards(matrix, pairing):
        rows, width = matrix.shape
        half = width // 2
        part = half // n_rows
        n_rounds = pairing.shape[0]
        raw_rows = sum(size for _, size in RAW)
        hbm = pl.BlockSpec(memory_space=pltpu.HBM)
        dma = pltpu.SemaphoreType.DMA

        def f32(*shape):
            return pltpu.VMEM(shape, F32)

        def bf16(*shape):
            return pltpu.VMEM(shape, BF16)

        return pl.pallas_call(
            functools.partial(kernel, n_wide, n_rows, n_rounds),
            out_shape=jax.ShapeDtypeStruct(matrix.shape, F32),
            in_specs=[hbm, hbm],
            out_specs=pl.BlockSpec(memory_space=pltpu.VMEM),
            scratch_shapes=[
                f32(rows, width),
                pltpu.VMEM(pairing.shape, pairing.dtype),
                f32(n_rounds, n_rows, part + 8, half),
                f32(n_rounds, n_rows, part + 8, half),
                f32(n_rounds, 8, 128),
                f32(n_rounds, 2 * n_rows, 8, 128),
                f32(n_rounds, part, half),
                f32(n_rounds, n_rows, part, half),
                f32(n_rounds, 8, 128),
                f32(n_rounds, n_wide // 2, 8, 128),
                f32(n_rounds, raw_rows, width),
                f32(n_rounds, raw_rows, width),
                f32(n_rounds, rows, half),
                f32(n_rounds, rows, half),
                f32(n_rounds, n_rows, part, half),
                f32(n_rounds, n_rows, part, half),
                f32(half, half),
                f32(n_rounds, rows, half),
                bf16(rows, width), bf16(rows, width),
                bf16(rows, half), bf16(rows, half), bf16(rows, half), bf16(rows, half),
                f32(half, half),
                f32(1, width),
                dma((CHUNKS,)), dma,
                dma((n_rounds,)), dma((n_rounds,)), dma((n_rounds,)), dma((n_rounds,)),
                dma((n_rounds,)), dma((n_rounds,)), dma((n_rounds,)), dma((n_rounds,)),
                dma((n_rounds, len(RAW))), dma((n_rounds, len(RAW))),
                dma((n_rounds, len(PIECES))), dma((n_rounds, len(PIECES))),
                dma((n_rounds, len(RELAY))), dma((n_rounds, len(RELAY))),
                dma((n_rounds, len(PIECES))), dma((n_rounds, len(PIECES))),
                dma((n_rounds,)), dma((n_rounds,)), dma((n_rounds,)), dma((n_rounds,)),
            ],
            compiler_params=pltpu.CompilerParams(
                collective_id=0, has_side_effects=True, vmem_limit_bytes=48 * 1024 * 1024
            ),
        )(matrix, pairing)

    return jax.shard_map(
        shards, mesh=mesh, in_specs=(P("rows", "wide"), P()), out_specs=P("rows", "wide"),
        check_vma=False,
    )
```

```python
import functools

import jax
import jax.numpy as jnp
from jax import lax
from jax.experimental import pallas as pl
from jax.experimental.pallas import tpu as pltpu
from jax.sharding import PartitionSpec as P

EPSILON = 1e-06
F32 = jnp.float32
BF16 = jnp.bfloat16
CHUNKS = 4
RAW = ((0, 256), (256, 192))
PIECES = ((448, 128), (576, 192), (768, 256))
EARLY = 2
RELAY = ((0, 256), (256, 192))
MESH = pl.DeviceIdType.MESH


def split(value):
    high = value.astype(BF16)
    low = (value - high.astype(F32)).astype(BF16)
    return high, low


def dot(left, right, dims=((1,), (0,))):
    return lax.dot_general(left, right, (dims, ((), ())), preferred_element_type=F32)


def mul(left, right, dims=((1,), (0,))):
    return (
        dot(left[0], right[0], dims)
        + dot(left[0], right[1], dims)
        + dot(left[1], right[0], dims)
    )


def total(value):
    return jnp.sum(jnp.sum(value, axis=0, keepdims=True), axis=1, keepdims=True)


def ring(distance, size):
    return min(distance, size - distance)


def row_peers(me_r, n_rows):
    n_y = n_rows // 2
    y, x = me_r // 2, me_r % 2
    offsets = [(dy, dx) for dy in range(n_y) for dx in range(2) if dy or dx]
    offsets.sort(key=lambda o: -(ring(o[0], n_y) + 2 * o[1]))
    return [((y + dy) % n_y) * 2 + (x + dx) % 2 for dy, dx in offsets]


def column_peers(me_w, n_wide):
    n_z = n_wide // 4
    x, z, core = me_w // (2 * n_z), (me_w // 2) % n_z, me_w % 2
    offsets = [(dz, dc) for dz in range(n_z) for dc in range(2) if dz or dc]
    offsets.sort(key=lambda o: -(ring(o[0], n_z) + 0.1 * o[1]))
    return [x * (2 * n_z) + ((z + dz) % n_z) * 2 + (core + dc) % 2 for dz, dc in offsets]


def wait(ref, sem):
    pltpu.make_async_copy(ref, ref, sem).wait()


def kernel(
    n_wide, n_rows, n_rounds,
    x_hbm, pairing_hbm, out_ref,
    x_ref, pairing_ref,
    gram_out, gram_in, part_out, parts, slice_out, slices, peak_out, peaks,
    raw_out, raw_in, v_out, v_in, behinds, crosses, cross, pass_in,
    cols_h, cols_l, u_h, u_l, v_h, v_l, gram_acc, norm_acc,
    x_sem, pairing_sem,
    gram_send, gram_recv, part_send, part_recv, slice_send, slice_recv, peak_send, peak_recv,
    raw_send, raw_recv, v_send, v_recv, relay_send, relay_recv, pass_send, pass_recv,
    c_send, c_recv, d_send, d_recv,
):
    rows, width = x_ref.shape
    half = width // 2
    part = half // n_rows
    step = rows // CHUNKS
    me_w = lax.axis_index("wide")
    me_r = lax.axis_index("rows")
    following = {"wide": lax.rem(me_w + 1, n_wide)}
    column = n_wide // 2
    first_z = lax.rem(me_w, column) == 0
    last_z = lax.rem(me_w, column) == column - 1
    next_z = {"wide": (me_w // column) * column + lax.rem(me_w + 1, column)}
    partner = {"wide": lax.rem(me_w + column, n_wide)}
    me_x, me_c = me_w // column, lax.rem(me_w, column)
    along_rows = [{"rows": peer} for peer in row_peers(me_r, n_rows)]
    along_column = [{"wide": peer} for peer in column_peers(me_w, n_wide)]

    def rows_of(pair):
        far = [{"wide": pair, "rows": device["rows"]} for device in along_rows]
        return far + [{"wide": pair, "rows": me_r}]


    def send(source, target, send_sem, recv_sem, device):
        pltpu.make_async_remote_copy(
            src_ref=source, dst_ref=target, send_sem=send_sem, recv_sem=recv_sem,
            device_id=device, device_id_type=MESH,
        ).start()

    pltpu.make_async_copy(pairing_hbm, pairing_ref, pairing_sem).start()
    for chunk in range(CHUNKS):
        at = pl.ds(chunk * step, step)
        pltpu.make_async_copy(x_hbm.at[at], x_ref.at[at], x_sem.at[chunk]).start()
    barrier = pltpu.get_barrier_semaphore()

    def greet(devices):
        for device in devices:
            pl.semaphore_signal(barrier, inc=1, device_id=device, device_id_type=MESH)

    known = along_rows + along_column + rows_of(partner["wide"])
    greet(known)

    @pl.when(last_z)
    def _():
        greet([following])

    @pl.when(first_z)
    def _():
        greet([{"wide": lax.rem(me_w + n_wide - 1, n_wide)}])


    eye = (
        lax.broadcasted_iota(jnp.int32, (half, half), 0)
        == lax.broadcasted_iota(jnp.int32, (half, half), 1)
    ).astype(F32)
    mine = (
        lax.broadcasted_iota(jnp.int32, (part, half), 0) + me_r * part
        == lax.broadcasted_iota(jnp.int32, (part, half), 1)
    )
    pltpu.make_async_copy(pairing_hbm, pairing_ref, pairing_sem).wait()
    factors = None
    raw_rows = sum(size for _, size in RAW)

    def send_raw(t, k):
        at = pl.ds(*RAW[k])
        send(raw_out.at[t, at], raw_in.at[t, at], raw_send.at[t, k], raw_recv.at[t, k], next_z)

    def finished(t, chunk):
        at = pl.ds(chunk * step, step)
        kept = mul((u_h[at, :], u_l[at, :]), factors[0])
        for k, (start, size) in enumerate(PIECES):
            if chunk * step <= start < (chunk + 1) * step:
                rows_at = pl.ds(start, size)
                wait(v_in.at[t, rows_at], v_recv.at[t, k])
                v_h[rows_at, :], v_l[rows_at, :] = split(v_in[t, rows_at, :])
        for k, (start, size) in enumerate(RELAY):
            if chunk * step <= start < (chunk + 1) * step:
                rows_at = pl.ds(start, size)

                @pl.when(first_z)
                def _():
                    wait(v_in.at[t, rows_at], relay_recv.at[t, k])
                    v_h[rows_at, :], v_l[rows_at, :] = split(v_in[t, rows_at, :])

        return jnp.concatenate([kept, mul((v_h[at, :], v_l[at, :]), factors[1])], axis=1)

    for t in range(n_rounds):
        order = (
            lax.broadcasted_iota(jnp.int32, (width, width), 0) == pairing_ref[t : t + 1, :]
        ).astype(BF16)
        gram_acc[...] = jnp.zeros_like(gram_acc)
        norm_acc[...] = jnp.zeros_like(norm_acc)
        for chunk in range(CHUNKS):
            at = pl.ds(chunk * step, step)
            if t == 0:
                pltpu.make_async_copy(x_hbm.at[at], x_ref.at[at], x_sem.at[chunk]).wait()
                block = x_ref[at, :]
            else:
                block = finished(t - 1, chunk)
            high, low = split(block)
            high = dot(high, order)
            low = dot(low, order)
            value = high + low
            if chunk * step < raw_rows:
                size = min(step, raw_rows - chunk * step)
                raw_out[t, pl.ds(chunk * step, size), :] = value[:size]
                if t > 0:
                    for k, (start, _) in enumerate(RAW):
                        if chunk * step <= start < (chunk + 1) * step:
                            send_raw(t, k)
            norm_acc[...] += jnp.sum(value * value, axis=0, keepdims=True)
            high, low = high.astype(BF16), low.astype(BF16)
            cols_h[at, :] = high
            cols_l[at, :] = low
            gram_acc[...] += mul(
                (high[:, :half], low[:, :half]), (high[:, half:], low[:, half:]), ((0,), (0,))
            )

        for k in range(n_rows):
            gram_out[t, k, 0:part, :] = gram_acc[k * part : (k + 1) * part, :]
            gram_out[t, k, part : part + 1, :] = norm_acc[:, :half]
            gram_out[t, k, part + 1 : part + 2, :] = norm_acc[:, half:]
        if t == 0:
            crossing = jnp.where(jnp.logical_or(first_z, last_z), 1, 0)
            pl.semaphore_wait(barrier, len(known) + crossing)
        for device in along_rows:
            send(
                gram_out.at[t, device["rows"]], gram_in.at[t, me_r],
                gram_send.at[t], gram_recv.at[t], device,
            )
        if t == 0:
            for k in range(len(RAW)):
                send_raw(t, k)
        gram_in[t, me_r] = gram_out[t, me_r]
        seven = pl.ds(0, n_rows - 1)
        all_but_one = pl.ds(0, 2 * n_rows - 1)
        wait(gram_in.at[t, seven], gram_recv.at[t])
        summed = gram_in[t, 0]
        for k in range(1, n_rows):
            summed = summed + gram_in[t, k]
        inverse_a = lax.rsqrt(summed[part : part + 1, :] + EPSILON)
        inverse_b = lax.rsqrt(summed[part + 1 : part + 2, :] + EPSILON)
        scaled = jnp.sum(jnp.where(mine, inverse_a, 0.0), axis=1, keepdims=True)
        share = summed[0:part, :] * scaled * inverse_b

        square = jnp.broadcast_to(total(share * share), (8, 128))
        part_out[t] = square
        place = me_x * n_rows + me_r
        parts[t, place] = square
        across = rows_of(partner["wide"])
        for device in across[:-1] + along_rows + across[-1:]:
            send(part_out.at[t], parts.at[t, place], part_send.at[t], part_recv.at[t], device)
        slice_out[t] = share
        slices[t, me_r] = share
        for device in along_rows:
            send(slice_out.at[t], slices.at[t, me_r], slice_send.at[t], slice_recv.at[t], device)
        wait(parts.at[t, all_but_one], part_recv.at[t])
        peak = parts[t, me_x * n_rows]
        other = parts[t, (1 - me_x) * n_rows]
        for k in range(1, n_rows):
            peak = peak + parts[t, me_x * n_rows + k]
            other = other + parts[t, (1 - me_x) * n_rows + k]
        own = peak[0:1, 0:1]
        peak = jnp.maximum(peak, other)
        peak_out[t] = peak
        peaks[t, me_c] = peak
        for device in along_column:
            send(peak_out.at[t], peaks.at[t, me_c], peak_send.at[t], peak_recv.at[t], device)

        wait(slices.at[t, seven], slice_recv.at[t])
        send(slices.at[t], behinds.at[t], c_send.at[t], c_recv.at[t], following)

        @pl.when(last_z)
        def _():
            send(slices.at[t], crosses.at[t], d_send.at[t], d_recv.at[t], next_z)

        coupling = slices[t].reshape(half, half)
        c = split(coupling)
        for k, (start, size) in enumerate(PIECES):
            at = pl.ds(start, size)
            high, low = cols_h[at, :], cols_l[at, :]
            v = high[:, half:].astype(F32) + low[:, half:].astype(F32)
            v_out[t, at, :] = v + mul((high[:, :half], low[:, :half]), c)

            @pl.when(last_z)
            def _():
                send(v_out.at[t, at], pass_in.at[t, at], pass_send.at[t, k], pass_recv.at[t, k], partner)


        wait(behinds.at[t], c_recv.at[t])
        behind = behinds[t].reshape(half, half)

        @pl.when(first_z)
        def _():
            wait(crosses.at[t], d_recv.at[t])
            cross[...] = crosses[t].reshape(half, half)

        @pl.when(jnp.logical_not(first_z))
        def _():
            cross[...] = behind

        c_cross = split(cross[...])
        for k, (start, size) in enumerate(RAW):
            at = pl.ds(start, size)
            wait(raw_in.at[t, at], raw_recv.at[t, k])
            left, right = raw_in[t, at, 0:half], raw_in[t, at, half:width]
            v = right + mul(split(left), c_cross)
            v_out[t, at, :] = v
            v_h[at, :], v_l[at, :] = split(v)

        @pl.when(first_z)
        def _():
            for k, (start, size) in enumerate(RELAY):
                at = pl.ds(start, size)
                send(v_out.at[t, at], v_in.at[t, at], relay_send.at[t, k], relay_recv.at[t, k], partner)

        ct = split(coupling.T)
        for chunk in range(CHUNKS):
            at = pl.ds(chunk * step, step)
            high, low = cols_h[at, :], cols_l[at, :]
            u = high[:, :half].astype(F32) + low[:, :half].astype(F32)
            u_h[at, :], u_l[at, :] = split(u - mul((high[:, half:], low[:, half:]), ct))

        def powers(left, right, bound):
            first = (eye + mul(left, right)) * (1.0 / (1.0 + bound))
            pieces = split(first)
            second = mul(pieces, pieces)
            return first, second, mul(split(second), pieces)

        kept_powers = powers(c, ct, own)
        c = split(behind)
        ct = split(behind.T)
        own_behind = total(behind * behind)
        moved_powers = powers(ct, c, own_behind)

        others = pl.ds(0, column - 1)
        wait(peaks.at[t, others], peak_recv.at[t])

        @pl.when(jnp.logical_not(last_z))
        def _():
            for k, (start, size) in enumerate(PIECES):
                at = pl.ds(start, size)
                send(v_out.at[t, at], v_in.at[t, at], v_send.at[t, k], v_recv.at[t, k], following)

        def forward(k):
            at = pl.ds(*PIECES[k])
            wait(pass_in.at[t, at], pass_recv.at[t, k])
            send(pass_in.at[t, at], v_in.at[t, at], v_send.at[t, k], v_recv.at[t, k], next_z)

        @pl.when(last_z)
        def _():
            for k in range(EARLY):
                forward(k)

        largest = jnp.max(peaks[t], axis=0)[0:1, 0:1]
        root = lax.rsqrt(1.0 + largest)
        factors = []
        for (first, second, third), bound in ((kept_powers, own), (moved_powers, own_behind)):
            ratio = (1.0 + bound) / (1.0 + largest)
            n1 = (2.25 * ratio) * first - (1.5 * ratio * ratio) * second
            n1 = n1 + (0.25 * ratio * ratio * ratio) * third
            t1 = split(1.5 * eye - 0.5 * n1)
            q1 = root * (1.5 * eye - (0.5 * ratio) * first)
            n2 = mul(split(mul(split(n1), t1)), t1)
            q2 = mul(split(q1), t1)
            t2 = split(1.5 * eye - 0.5 * n2)
            factors.append(split(mul(split(q2), t2)))

        @pl.when(last_z)
        def _():
            for k in range(EARLY, len(PIECES)):
                forward(k)

    for chunk in range(CHUNKS):
        at = pl.ds(chunk * step, step)
        out_ref[at, :] = finished(n_rounds - 1, chunk)

    for t in range(n_rounds):
        wait(gram_out.at[t, seven], gram_send.at[t])
        wait(parts.at[t, all_but_one], part_send.at[t])
        wait(slices.at[t, seven], slice_send.at[t])
        wait(peaks.at[t, others], peak_send.at[t])
        wait(behinds.at[t], c_send.at[t])
        for k, (start, size) in enumerate(RAW):
            wait(raw_out.at[t, pl.ds(start, size)], raw_send.at[t, k])
        for k, (start, size) in enumerate(PIECES):
            wait(v_out.at[t, pl.ds(start, size)], v_send.at[t, k])

        @pl.when(last_z)
        def _():
            wait(crosses.at[t], d_send.at[t])
            for k, (start, size) in enumerate(PIECES):
                wait(v_out.at[t, pl.ds(start, size)], pass_send.at[t, k])

        @pl.when(first_z)
        def _():
            for k, (start, size) in enumerate(RELAY):
                wait(v_out.at[t, pl.ds(start, size)], relay_send.at[t, k])


def solution(mesh):
    n_wide, n_rows = mesh.shape["wide"], mesh.shape["rows"]

    def shards(matrix, pairing):
        rows, width = matrix.shape
        half = width // 2
        part = half // n_rows
        n_rounds = pairing.shape[0]
        raw_rows = sum(size for _, size in RAW)
        hbm = pl.BlockSpec(memory_space=pltpu.HBM)
        dma = pltpu.SemaphoreType.DMA

        def f32(*shape):
            return pltpu.VMEM(shape, F32)

        def bf16(*shape):
            return pltpu.VMEM(shape, BF16)

        return pl.pallas_call(
            functools.partial(kernel, n_wide, n_rows, n_rounds),
            out_shape=jax.ShapeDtypeStruct(matrix.shape, F32),
            in_specs=[hbm, hbm],
            out_specs=pl.BlockSpec(memory_space=pltpu.VMEM),
            scratch_shapes=[
                f32(rows, width),
                pltpu.VMEM(pairing.shape, pairing.dtype),
                f32(n_rounds, n_rows, part + 8, half),
                f32(n_rounds, n_rows, part + 8, half),
                f32(n_rounds, 8, 128),
                f32(n_rounds, 2 * n_rows, 8, 128),
                f32(n_rounds, part, half),
                f32(n_rounds, n_rows, part, half),
                f32(n_rounds, 8, 128),
                f32(n_rounds, n_wide // 2, 8, 128),
                f32(n_rounds, raw_rows, width),
                f32(n_rounds, raw_rows, width),
                f32(n_rounds, rows, half),
                f32(n_rounds, rows, half),
                f32(n_rounds, n_rows, part, half),
                f32(n_rounds, n_rows, part, half),
                f32(half, half),
                f32(n_rounds, rows, half),
                bf16(rows, width), bf16(rows, width),
                bf16(rows, half), bf16(rows, half), bf16(rows, half), bf16(rows, half),
                f32(half, half),
                f32(1, width),
                dma((CHUNKS,)), dma,
                dma((n_rounds,)), dma((n_rounds,)), dma((n_rounds,)), dma((n_rounds,)),
                dma((n_rounds,)), dma((n_rounds,)), dma((n_rounds,)), dma((n_rounds,)),
                dma((n_rounds, len(RAW))), dma((n_rounds, len(RAW))),
                dma((n_rounds, len(PIECES))), dma((n_rounds, len(PIECES))),
                dma((n_rounds, len(RELAY))), dma((n_rounds, len(RELAY))),
                dma((n_rounds, len(PIECES))), dma((n_rounds, len(PIECES))),
                dma((n_rounds,)), dma((n_rounds,)), dma((n_rounds,)), dma((n_rounds,)),
            ],
            compiler_params=pltpu.CompilerParams(
                collective_id=0, has_side_effects=True, vmem_limit_bytes=48 * 1024 * 1024
            ),
        )(matrix, pairing)

    return jax.shard_map(
        shards, mesh=mesh, in_specs=(P("rows", "wide"), P()), out_specs=P("rows", "wide"),
        check_vma=False,
    )
```

```python
import functools

import jax
import jax.numpy as jnp
from jax import lax
from jax.experimental import pallas as pl
from jax.experimental.pallas import tpu as pltpu
from jax.sharding import PartitionSpec as P

EPSILON = 1e-06
F32 = jnp.float32
BF16 = jnp.bfloat16
CHUNKS = 4
RAW = ((0, 256), (256, 192))
PIECES = ((448, 128), (576, 192), (768, 256))
EARLY = 3
RELAY = ((0, 256), (256, 192))
MESH = pl.DeviceIdType.MESH


def split(value):
    high = value.astype(BF16)
    low = (value - high.astype(F32)).astype(BF16)
    return high, low


def dot(left, right, dims=((1,), (0,))):
    return lax.dot_general(left, right, (dims, ((), ())), preferred_element_type=F32)


def mul(left, right, dims=((1,), (0,))):
    return (
        dot(left[0], right[0], dims)
        + dot(left[0], right[1], dims)
        + dot(left[1], right[0], dims)
    )


def total(value):
    return jnp.sum(jnp.sum(value, axis=0, keepdims=True), axis=1, keepdims=True)


def ring(distance, size):
    return min(distance, size - distance)


def row_peers(me_r, n_rows):
    n_y = n_rows // 2
    y, x = me_r // 2, me_r % 2
    offsets = [(dy, dx) for dy in range(n_y) for dx in range(2) if dy or dx]
    offsets.sort(key=lambda o: -(ring(o[0], n_y) + 2 * o[1]))
    return [((y + dy) % n_y) * 2 + (x + dx) % 2 for dy, dx in offsets]


def column_peers(me_w, n_wide):
    n_z = n_wide // 4
    x, z, core = me_w // (2 * n_z), (me_w // 2) % n_z, me_w % 2
    offsets = [(dz, dc) for dz in range(n_z) for dc in range(2) if dz or dc]
    offsets.sort(key=lambda o: -(ring(o[0], n_z) + 0.1 * o[1]))
    return [x * (2 * n_z) + ((z + dz) % n_z) * 2 + (core + dc) % 2 for dz, dc in offsets]


def wait(ref, sem):
    pltpu.make_async_copy(ref, ref, sem).wait()


def kernel(
    n_wide, n_rows, n_rounds,
    x_hbm, pairing_hbm, out_ref,
    x_ref, pairing_ref,
    gram_out, gram_in, part_out, parts, slice_out, slices, peak_out, peaks,
    raw_out, raw_in, v_out, v_in, behinds, crosses, cross, pass_in,
    cols_h, cols_l, u_h, u_l, v_h, v_l, gram_acc, norm_acc,
    x_sem, pairing_sem,
    gram_send, gram_recv, part_send, part_recv, slice_send, slice_recv, peak_send, peak_recv,
    raw_send, raw_recv, v_send, v_recv, relay_send, relay_recv, pass_send, pass_recv,
    c_send, c_recv, d_send, d_recv,
):
    rows, width = x_ref.shape
    half = width // 2
    part = half // n_rows
    step = rows // CHUNKS
    me_w = lax.axis_index("wide")
    me_r = lax.axis_index("rows")
    following = {"wide": lax.rem(me_w + 1, n_wide)}
    column = n_wide // 2
    first_z = lax.rem(me_w, column) == 0
    last_z = lax.rem(me_w, column) == column - 1
    next_z = {"wide": (me_w // column) * column + lax.rem(me_w + 1, column)}
    partner = {"wide": lax.rem(me_w + column, n_wide)}
    me_x, me_c = me_w // column, lax.rem(me_w, column)
    along_rows = [{"rows": peer} for peer in row_peers(me_r, n_rows)]
    along_column = [{"wide": peer} for peer in column_peers(me_w, n_wide)]

    def rows_of(pair):
        far = [{"wide": pair, "rows": device["rows"]} for device in along_rows]
        return far + [{"wide": pair, "rows": me_r}]


    def send(source, target, send_sem, recv_sem, device):
        pltpu.make_async_remote_copy(
            src_ref=source, dst_ref=target, send_sem=send_sem, recv_sem=recv_sem,
            device_id=device, device_id_type=MESH,
        ).start()

    pltpu.make_async_copy(pairing_hbm, pairing_ref, pairing_sem).start()
    for chunk in range(CHUNKS):
        at = pl.ds(chunk * step, step)
        pltpu.make_async_copy(x_hbm.at[at], x_ref.at[at], x_sem.at[chunk]).start()
    barrier = pltpu.get_barrier_semaphore()

    def greet(devices):
        for device in devices:
            pl.semaphore_signal(barrier, inc=1, device_id=device, device_id_type=MESH)

    known = along_rows + along_column + rows_of(partner["wide"])
    greet(known)

    @pl.when(last_z)
    def _():
        greet([following])

    @pl.when(first_z)
    def _():
        greet([{"wide": lax.rem(me_w + n_wide - 1, n_wide)}])


    eye = (
        lax.broadcasted_iota(jnp.int32, (half, half), 0)
        == lax.broadcasted_iota(jnp.int32, (half, half), 1)
    ).astype(F32)
    mine = (
        lax.broadcasted_iota(jnp.int32, (part, half), 0) + me_r * part
        == lax.broadcasted_iota(jnp.int32, (part, half), 1)
    )
    pltpu.make_async_copy(pairing_hbm, pairing_ref, pairing_sem).wait()
    factors = None
    raw_rows = sum(size for _, size in RAW)

    def send_raw(t, k):
        at = pl.ds(*RAW[k])
        send(raw_out.at[t, at], raw_in.at[t, at], raw_send.at[t, k], raw_recv.at[t, k], next_z)

    def finished(t, chunk):
        at = pl.ds(chunk * step, step)
        kept = mul((u_h[at, :], u_l[at, :]), factors[0])
        for k, (start, size) in enumerate(PIECES):
            if chunk * step <= start < (chunk + 1) * step:
                rows_at = pl.ds(start, size)
                wait(v_in.at[t, rows_at], v_recv.at[t, k])
                v_h[rows_at, :], v_l[rows_at, :] = split(v_in[t, rows_at, :])
        for k, (start, size) in enumerate(RELAY):
            if chunk * step <= start < (chunk + 1) * step:
                rows_at = pl.ds(start, size)

                @pl.when(first_z)
                def _():
                    wait(v_in.at[t, rows_at], relay_recv.at[t, k])
                    v_h[rows_at, :], v_l[rows_at, :] = split(v_in[t, rows_at, :])

        return jnp.concatenate([kept, mul((v_h[at, :], v_l[at, :]), factors[1])], axis=1)

    for t in range(n_rounds):
        order = (
            lax.broadcasted_iota(jnp.int32, (width, width), 0) == pairing_ref[t : t + 1, :]
        ).astype(BF16)
        gram_acc[...] = jnp.zeros_like(gram_acc)
        norm_acc[...] = jnp.zeros_like(norm_acc)
        for chunk in range(CHUNKS):
            at = pl.ds(chunk * step, step)
            if t == 0:
                pltpu.make_async_copy(x_hbm.at[at], x_ref.at[at], x_sem.at[chunk]).wait()
                block = x_ref[at, :]
            else:
                block = finished(t - 1, chunk)
            high, low = split(block)
            high = dot(high, order)
            low = dot(low, order)
            value = high + low
            if chunk * step < raw_rows:
                size = min(step, raw_rows - chunk * step)
                raw_out[t, pl.ds(chunk * step, size), :] = value[:size]
                if t > 0:
                    for k, (start, _) in enumerate(RAW):
                        if chunk * step <= start < (chunk + 1) * step:
                            send_raw(t, k)
            norm_acc[...] += jnp.sum(value * value, axis=0, keepdims=True)
            high, low = high.astype(BF16), low.astype(BF16)
            cols_h[at, :] = high
            cols_l[at, :] = low
            gram_acc[...] += mul(
                (high[:, :half], low[:, :half]), (high[:, half:], low[:, half:]), ((0,), (0,))
            )

        for k in range(n_rows):
            gram_out[t, k, 0:part, :] = gram_acc[k * part : (k + 1) * part, :]
            gram_out[t, k, part : part + 1, :] = norm_acc[:, :half]
            gram_out[t, k, part + 1 : part + 2, :] = norm_acc[:, half:]
        if t == 0:
            crossing = jnp.where(jnp.logical_or(first_z, last_z), 1, 0)
            pl.semaphore_wait(barrier, len(known) + crossing)
        for device in along_rows:
            send(
                gram_out.at[t, device["rows"]], gram_in.at[t, me_r],
                gram_send.at[t], gram_recv.at[t], device,
            )
        if t == 0:
            for k in range(len(RAW)):
                send_raw(t, k)
        gram_in[t, me_r] = gram_out[t, me_r]
        seven = pl.ds(0, n_rows - 1)
        all_but_one = pl.ds(0, 2 * n_rows - 1)
        wait(gram_in.at[t, seven], gram_recv.at[t])
        summed = gram_in[t, 0]
        for k in range(1, n_rows):
            summed = summed + gram_in[t, k]
        inverse_a = lax.rsqrt(summed[part : part + 1, :] + EPSILON)
        inverse_b = lax.rsqrt(summed[part + 1 : part + 2, :] + EPSILON)
        scaled = jnp.sum(jnp.where(mine, inverse_a, 0.0), axis=1, keepdims=True)
        share = summed[0:part, :] * scaled * inverse_b

        square = jnp.broadcast_to(total(share * share), (8, 128))
        part_out[t] = square
        place = me_x * n_rows + me_r
        parts[t, place] = square
        across = rows_of(partner["wide"])
        for device in across[:-1] + along_rows + across[-1:]:
            send(part_out.at[t], parts.at[t, place], part_send.at[t], part_recv.at[t], device)
        slice_out[t] = share
        slices[t, me_r] = share
        for device in along_rows:
            send(slice_out.at[t], slices.at[t, me_r], slice_send.at[t], slice_recv.at[t], device)
        wait(parts.at[t, all_but_one], part_recv.at[t])
        peak = parts[t, me_x * n_rows]
        other = parts[t, (1 - me_x) * n_rows]
        for k in range(1, n_rows):
            peak = peak + parts[t, me_x * n_rows + k]
            other = other + parts[t, (1 - me_x) * n_rows + k]
        own = peak[0:1, 0:1]
        peak = jnp.maximum(peak, other)
        peak_out[t] = peak
        peaks[t, me_c] = peak
        for device in along_column:
            send(peak_out.at[t], peaks.at[t, me_c], peak_send.at[t], peak_recv.at[t], device)

        wait(slices.at[t, seven], slice_recv.at[t])
        send(slices.at[t], behinds.at[t], c_send.at[t], c_recv.at[t], following)

        @pl.when(last_z)
        def _():
            send(slices.at[t], crosses.at[t], d_send.at[t], d_recv.at[t], next_z)

        coupling = slices[t].reshape(half, half)
        c = split(coupling)
        for k, (start, size) in enumerate(PIECES):
            at = pl.ds(start, size)
            high, low = cols_h[at, :], cols_l[at, :]
            v = high[:, half:].astype(F32) + low[:, half:].astype(F32)
            v_out[t, at, :] = v + mul((high[:, :half], low[:, :half]), c)

            @pl.when(last_z)
            def _():
                send(v_out.at[t, at], pass_in.at[t, at], pass_send.at[t, k], pass_recv.at[t, k], partner)


        wait(behinds.at[t], c_recv.at[t])
        behind = behinds[t].reshape(half, half)

        @pl.when(first_z)
        def _():
            wait(crosses.at[t], d_recv.at[t])
            cross[...] = crosses[t].reshape(half, half)

        @pl.when(jnp.logical_not(first_z))
        def _():
            cross[...] = behind

        c_cross = split(cross[...])
        for k, (start, size) in enumerate(RAW):
            at = pl.ds(start, size)
            wait(raw_in.at[t, at], raw_recv.at[t, k])
            left, right = raw_in[t, at, 0:half], raw_in[t, at, half:width]
            v = right + mul(split(left), c_cross)
            v_out[t, at, :] = v
            v_h[at, :], v_l[at, :] = split(v)

        @pl.when(first_z)
        def _():
            for k, (start, size) in enumerate(RELAY):
                at = pl.ds(start, size)
                send(v_out.at[t, at], v_in.at[t, at], relay_send.at[t, k], relay_recv.at[t, k], partner)

        ct = split(coupling.T)
        for chunk in range(CHUNKS):
            at = pl.ds(chunk * step, step)
            high, low = cols_h[at, :], cols_l[at, :]
            u = high[:, :half].astype(F32) + low[:, :half].astype(F32)
            u_h[at, :], u_l[at, :] = split(u - mul((high[:, half:], low[:, half:]), ct))

        def powers(left, right, bound):
            first = (eye + mul(left, right)) * (1.0 / (1.0 + bound))
            pieces = split(first)
            second = mul(pieces, pieces)
            return first, second, mul(split(second), pieces)

        kept_powers = powers(c, ct, own)
        c = split(behind)
        ct = split(behind.T)
        own_behind = total(behind * behind)
        moved_powers = powers(ct, c, own_behind)

        others = pl.ds(0, column - 1)
        wait(peaks.at[t, others], peak_recv.at[t])

        @pl.when(jnp.logical_not(last_z))
        def _():
            for k, (start, size) in enumerate(PIECES):
                at = pl.ds(start, size)
                send(v_out.at[t, at], v_in.at[t, at], v_send.at[t, k], v_recv.at[t, k], following)

        def forward(k):
            at = pl.ds(*PIECES[k])
            wait(pass_in.at[t, at], pass_recv.at[t, k])
            send(pass_in.at[t, at], v_in.at[t, at], v_send.at[t, k], v_recv.at[t, k], next_z)

        @pl.when(last_z)
        def _():
            for k in range(EARLY):
                forward(k)

        largest = jnp.max(peaks[t], axis=0)[0:1, 0:1]
        root = lax.rsqrt(1.0 + largest)
        factors = []
        for (first, second, third), bound in ((kept_powers, own), (moved_powers, own_behind)):
            ratio = (1.0 + bound) / (1.0 + largest)
            n1 = (2.25 * ratio) * first - (1.5 * ratio * ratio) * second
            n1 = n1 + (0.25 * ratio * ratio * ratio) * third
            t1 = split(1.5 * eye - 0.5 * n1)
            q1 = root * (1.5 * eye - (0.5 * ratio) * first)
            n2 = mul(split(mul(split(n1), t1)), t1)
            q2 = mul(split(q1), t1)
            t2 = split(1.5 * eye - 0.5 * n2)
            factors.append(split(mul(split(q2), t2)))

        @pl.when(last_z)
        def _():
            for k in range(EARLY, len(PIECES)):
                forward(k)

    for chunk in range(CHUNKS):
        at = pl.ds(chunk * step, step)
        out_ref[at, :] = finished(n_rounds - 1, chunk)

    for t in range(n_rounds):
        wait(gram_out.at[t, seven], gram_send.at[t])
        wait(parts.at[t, all_but_one], part_send.at[t])
        wait(slices.at[t, seven], slice_send.at[t])
        wait(peaks.at[t, others], peak_send.at[t])
        wait(behinds.at[t], c_send.at[t])
        for k, (start, size) in enumerate(RAW):
            wait(raw_out.at[t, pl.ds(start, size)], raw_send.at[t, k])
        for k, (start, size) in enumerate(PIECES):
            wait(v_out.at[t, pl.ds(start, size)], v_send.at[t, k])

        @pl.when(last_z)
        def _():
            wait(crosses.at[t], d_send.at[t])
            for k, (start, size) in enumerate(PIECES):
                wait(v_out.at[t, pl.ds(start, size)], pass_send.at[t, k])

        @pl.when(first_z)
        def _():
            for k, (start, size) in enumerate(RELAY):
                wait(v_out.at[t, pl.ds(start, size)], relay_send.at[t, k])


def solution(mesh):
    n_wide, n_rows = mesh.shape["wide"], mesh.shape["rows"]

    def shards(matrix, pairing):
        rows, width = matrix.shape
        half = width // 2
        part = half // n_rows
        n_rounds = pairing.shape[0]
        raw_rows = sum(size for _, size in RAW)
        hbm = pl.BlockSpec(memory_space=pltpu.HBM)
        dma = pltpu.SemaphoreType.DMA

        def f32(*shape):
            return pltpu.VMEM(shape, F32)

        def bf16(*shape):
            return pltpu.VMEM(shape, BF16)

        return pl.pallas_call(
            functools.partial(kernel, n_wide, n_rows, n_rounds),
            out_shape=jax.ShapeDtypeStruct(matrix.shape, F32),
            in_specs=[hbm, hbm],
            out_specs=pl.BlockSpec(memory_space=pltpu.VMEM),
            scratch_shapes=[
                f32(rows, width),
                pltpu.VMEM(pairing.shape, pairing.dtype),
                f32(n_rounds, n_rows, part + 8, half),
                f32(n_rounds, n_rows, part + 8, half),
                f32(n_rounds, 8, 128),
                f32(n_rounds, 2 * n_rows, 8, 128),
                f32(n_rounds, part, half),
                f32(n_rounds, n_rows, part, half),
                f32(n_rounds, 8, 128),
                f32(n_rounds, n_wide // 2, 8, 128),
                f32(n_rounds, raw_rows, width),
                f32(n_rounds, raw_rows, width),
                f32(n_rounds, rows, half),
                f32(n_rounds, rows, half),
                f32(n_rounds, n_rows, part, half),
                f32(n_rounds, n_rows, part, half),
                f32(half, half),
                f32(n_rounds, rows, half),
                bf16(rows, width), bf16(rows, width),
                bf16(rows, half), bf16(rows, half), bf16(rows, half), bf16(rows, half),
                f32(half, half),
                f32(1, width),
                dma((CHUNKS,)), dma,
                dma((n_rounds,)), dma((n_rounds,)), dma((n_rounds,)), dma((n_rounds,)),
                dma((n_rounds,)), dma((n_rounds,)), dma((n_rounds,)), dma((n_rounds,)),
                dma((n_rounds, len(RAW))), dma((n_rounds, len(RAW))),
                dma((n_rounds, len(PIECES))), dma((n_rounds, len(PIECES))),
                dma((n_rounds, len(RELAY))), dma((n_rounds, len(RELAY))),
                dma((n_rounds, len(PIECES))), dma((n_rounds, len(PIECES))),
                dma((n_rounds,)), dma((n_rounds,)), dma((n_rounds,)), dma((n_rounds,)),
            ],
            compiler_params=pltpu.CompilerParams(
                collective_id=0, has_side_effects=True, vmem_limit_bytes=48 * 1024 * 1024
            ),
        )(matrix, pairing)

    return jax.shard_map(
        shards, mesh=mesh, in_specs=(P("rows", "wide"), P()), out_specs=P("rows", "wide"),
        check_vma=False,
    )
```

```python
import functools

import jax
import jax.numpy as jnp
from jax import lax
from jax.experimental import pallas as pl
from jax.experimental.pallas import tpu as pltpu
from jax.sharding import PartitionSpec as P

EPSILON = 1e-06
F32 = jnp.float32
BF16 = jnp.bfloat16
CHUNKS = 4
RAW = ((0, 256), (256, 192))
PIECES = ((448, 128), (576, 192), (768, 256))
EARLY = 1
RELAY = ((0, 256), (256, 192))
MESH = pl.DeviceIdType.MESH


def split(value):
    high = value.astype(BF16)
    low = (value - high.astype(F32)).astype(BF16)
    return high, low


def dot(left, right, dims=((1,), (0,))):
    return lax.dot_general(left, right, (dims, ((), ())), preferred_element_type=F32)


def mul(left, right, dims=((1,), (0,))):
    return (
        dot(left[0], right[0], dims)
        + dot(left[0], right[1], dims)
        + dot(left[1], right[0], dims)
    )


def total(value):
    return jnp.sum(jnp.sum(value, axis=0, keepdims=True), axis=1, keepdims=True)


def ring(distance, size):
    return min(distance, size - distance)


def row_peers(me_r, n_rows):
    n_y = n_rows // 2
    y, x = me_r // 2, me_r % 2
    offsets = [(dy, dx) for dy in range(n_y) for dx in range(2) if dy or dx]
    offsets.sort(key=lambda o: -(ring(o[0], n_y) + 2 * o[1]))
    return [((y + dy) % n_y) * 2 + (x + dx) % 2 for dy, dx in offsets]


def column_peers(me_w, n_wide):
    n_z = n_wide // 4
    x, z, core = me_w // (2 * n_z), (me_w // 2) % n_z, me_w % 2
    offsets = [(dz, dc) for dz in range(n_z) for dc in range(2) if dz or dc]
    offsets.sort(key=lambda o: -(ring(o[0], n_z) + 0.1 * o[1]))
    return [x * (2 * n_z) + ((z + dz) % n_z) * 2 + (core + dc) % 2 for dz, dc in offsets]


def wait(ref, sem):
    pltpu.make_async_copy(ref, ref, sem).wait()


def kernel(
    n_wide, n_rows, n_rounds,
    x_hbm, pairing_hbm, out_ref,
    x_ref, pairing_ref,
    gram_out, gram_in, part_out, parts, slice_out, slices, peak_out, peaks,
    raw_out, raw_in, v_out, v_in, behinds, crosses, cross, pass_in,
    cols_h, cols_l, u_h, u_l, v_h, v_l, gram_acc, norm_acc,
    x_sem, pairing_sem,
    gram_send, gram_recv, part_send, part_recv, slice_send, slice_recv, peak_send, peak_recv,
    raw_send, raw_recv, v_send, v_recv, relay_send, relay_recv, pass_send, pass_recv,
    c_send, c_recv, d_send, d_recv,
):
    rows, width = x_ref.shape
    half = width // 2
    part = half // n_rows
    step = rows // CHUNKS
    me_w = lax.axis_index("wide")
    me_r = lax.axis_index("rows")
    following = {"wide": lax.rem(me_w + 1, n_wide)}
    column = n_wide // 2
    first_z = lax.rem(me_w, column) == 0
    last_z = lax.rem(me_w, column) == column - 1
    next_z = {"wide": (me_w // column) * column + lax.rem(me_w + 1, column)}
    partner = {"wide": lax.rem(me_w + column, n_wide)}
    me_x, me_c = me_w // column, lax.rem(me_w, column)
    along_rows = [{"rows": peer} for peer in row_peers(me_r, n_rows)]
    along_column = [{"wide": peer} for peer in column_peers(me_w, n_wide)]

    def rows_of(pair):
        far = [{"wide": pair, "rows": device["rows"]} for device in along_rows]
        return far + [{"wide": pair, "rows": me_r}]


    def send(source, target, send_sem, recv_sem, device):
        pltpu.make_async_remote_copy(
            src_ref=source, dst_ref=target, send_sem=send_sem, recv_sem=recv_sem,
            device_id=device, device_id_type=MESH,
        ).start()

    pltpu.make_async_copy(pairing_hbm, pairing_ref, pairing_sem).start()
    for chunk in range(CHUNKS):
        at = pl.ds(chunk * step, step)
        pltpu.make_async_copy(x_hbm.at[at], x_ref.at[at], x_sem.at[chunk]).start()
    barrier = pltpu.get_barrier_semaphore()

    def greet(devices):
        for device in devices:
            pl.semaphore_signal(barrier, inc=1, device_id=device, device_id_type=MESH)

    known = along_rows + along_column + rows_of(partner["wide"])
    greet(known)

    @pl.when(last_z)
    def _():
        greet([following])

    @pl.when(first_z)
    def _():
        greet([{"wide": lax.rem(me_w + n_wide - 1, n_wide)}])


    eye = (
        lax.broadcasted_iota(jnp.int32, (half, half), 0)
        == lax.broadcasted_iota(jnp.int32, (half, half), 1)
    ).astype(F32)
    mine = (
        lax.broadcasted_iota(jnp.int32, (part, half), 0) + me_r * part
        == lax.broadcasted_iota(jnp.int32, (part, half), 1)
    )
    pltpu.make_async_copy(pairing_hbm, pairing_ref, pairing_sem).wait()
    factors = None
    raw_rows = sum(size for _, size in RAW)

    def send_raw(t, k):
        at = pl.ds(*RAW[k])
        send(raw_out.at[t, at], raw_in.at[t, at], raw_send.at[t, k], raw_recv.at[t, k], next_z)

    def finished(t, chunk):
        at = pl.ds(chunk * step, step)
        kept = mul((u_h[at, :], u_l[at, :]), factors[0])
        for k, (start, size) in enumerate(PIECES):
            if chunk * step <= start < (chunk + 1) * step:
                rows_at = pl.ds(start, size)
                wait(v_in.at[t, rows_at], v_recv.at[t, k])
                v_h[rows_at, :], v_l[rows_at, :] = split(v_in[t, rows_at, :])
        for k, (start, size) in enumerate(RELAY):
            if chunk * step <= start < (chunk + 1) * step:
                rows_at = pl.ds(start, size)

                @pl.when(first_z)
                def _():
                    wait(v_in.at[t, rows_at], relay_recv.at[t, k])
                    v_h[rows_at, :], v_l[rows_at, :] = split(v_in[t, rows_at, :])

        return jnp.concatenate([kept, mul((v_h[at, :], v_l[at, :]), factors[1])], axis=1)

    for t in range(n_rounds):
        order = (
            lax.broadcasted_iota(jnp.int32, (width, width), 0) == pairing_ref[t : t + 1, :]
        ).astype(BF16)
        gram_acc[...] = jnp.zeros_like(gram_acc)
        norm_acc[...] = jnp.zeros_like(norm_acc)
        for chunk in range(CHUNKS):
            at = pl.ds(chunk * step, step)
            if t == 0:
                pltpu.make_async_copy(x_hbm.at[at], x_ref.at[at], x_sem.at[chunk]).wait()
                block = x_ref[at, :]
            else:
                block = finished(t - 1, chunk)
            high, low = split(block)
            high = dot(high, order)
            low = dot(low, order)
            value = high + low
            if chunk * step < raw_rows:
                size = min(step, raw_rows - chunk * step)
                raw_out[t, pl.ds(chunk * step, size), :] = value[:size]
                if t > 0:
                    for k, (start, _) in enumerate(RAW):
                        if chunk * step <= start < (chunk + 1) * step:
                            send_raw(t, k)
            norm_acc[...] += jnp.sum(value * value, axis=0, keepdims=True)
            high, low = high.astype(BF16), low.astype(BF16)
            cols_h[at, :] = high
            cols_l[at, :] = low
            gram_acc[...] += mul(
                (high[:, :half], low[:, :half]), (high[:, half:], low[:, half:]), ((0,), (0,))
            )

        for k in range(n_rows):
            gram_out[t, k, 0:part, :] = gram_acc[k * part : (k + 1) * part, :]
            gram_out[t, k, part : part + 1, :] = norm_acc[:, :half]
            gram_out[t, k, part + 1 : part + 2, :] = norm_acc[:, half:]
        if t == 0:
            crossing = jnp.where(jnp.logical_or(first_z, last_z), 1, 0)
            pl.semaphore_wait(barrier, len(known) + crossing)
        for device in along_rows:
            send(
                gram_out.at[t, device["rows"]], gram_in.at[t, me_r],
                gram_send.at[t], gram_recv.at[t], device,
            )
        if t == 0:
            for k in range(len(RAW)):
                send_raw(t, k)
        gram_in[t, me_r] = gram_out[t, me_r]
        seven = pl.ds(0, n_rows - 1)
        all_but_one = pl.ds(0, 2 * n_rows - 1)
        wait(gram_in.at[t, seven], gram_recv.at[t])
        summed = gram_in[t, 0]
        for k in range(1, n_rows):
            summed = summed + gram_in[t, k]
        inverse_a = lax.rsqrt(summed[part : part + 1, :] + EPSILON)
        inverse_b = lax.rsqrt(summed[part + 1 : part + 2, :] + EPSILON)
        scaled = jnp.sum(jnp.where(mine, inverse_a, 0.0), axis=1, keepdims=True)
        share = summed[0:part, :] * scaled * inverse_b

        square = jnp.broadcast_to(total(share * share), (8, 128))
        part_out[t] = square
        place = me_x * n_rows + me_r
        parts[t, place] = square
        across = rows_of(partner["wide"])
        for device in across[:-1] + along_rows + across[-1:]:
            send(part_out.at[t], parts.at[t, place], part_send.at[t], part_recv.at[t], device)
        slice_out[t] = share
        slices[t, me_r] = share
        for device in along_rows:
            send(slice_out.at[t], slices.at[t, me_r], slice_send.at[t], slice_recv.at[t], device)
        wait(parts.at[t, all_but_one], part_recv.at[t])
        peak = parts[t, me_x * n_rows]
        other = parts[t, (1 - me_x) * n_rows]
        for k in range(1, n_rows):
            peak = peak + parts[t, me_x * n_rows + k]
            other = other + parts[t, (1 - me_x) * n_rows + k]
        own = peak[0:1, 0:1]
        peak = jnp.maximum(peak, other)
        peak_out[t] = peak
        peaks[t, me_c] = peak
        for device in along_column:
            send(peak_out.at[t], peaks.at[t, me_c], peak_send.at[t], peak_recv.at[t], device)

        wait(slices.at[t, seven], slice_recv.at[t])
        send(slices.at[t], behinds.at[t], c_send.at[t], c_recv.at[t], following)

        @pl.when(last_z)
        def _():
            send(slices.at[t], crosses.at[t], d_send.at[t], d_recv.at[t], next_z)

        coupling = slices[t].reshape(half, half)
        c = split(coupling)
        for k, (start, size) in enumerate(PIECES):
            at = pl.ds(start, size)
            high, low = cols_h[at, :], cols_l[at, :]
            v = high[:, half:].astype(F32) + low[:, half:].astype(F32)
            v_out[t, at, :] = v + mul((high[:, :half], low[:, :half]), c)

            @pl.when(last_z)
            def _():
                send(v_out.at[t, at], pass_in.at[t, at], pass_send.at[t, k], pass_recv.at[t, k], partner)


        wait(behinds.at[t], c_recv.at[t])
        behind = behinds[t].reshape(half, half)

        @pl.when(first_z)
        def _():
            wait(crosses.at[t], d_recv.at[t])
            cross[...] = crosses[t].reshape(half, half)

        @pl.when(jnp.logical_not(first_z))
        def _():
            cross[...] = behind

        c_cross = split(cross[...])
        for k, (start, size) in enumerate(RAW):
            at = pl.ds(start, size)
            wait(raw_in.at[t, at], raw_recv.at[t, k])
            left, right = raw_in[t, at, 0:half], raw_in[t, at, half:width]
            v = right + mul(split(left), c_cross)
            v_out[t, at, :] = v
            v_h[at, :], v_l[at, :] = split(v)

        @pl.when(first_z)
        def _():
            for k, (start, size) in enumerate(RELAY):
                at = pl.ds(start, size)
                send(v_out.at[t, at], v_in.at[t, at], relay_send.at[t, k], relay_recv.at[t, k], partner)

        ct = split(coupling.T)
        for chunk in range(CHUNKS):
            at = pl.ds(chunk * step, step)
            high, low = cols_h[at, :], cols_l[at, :]
            u = high[:, :half].astype(F32) + low[:, :half].astype(F32)
            u_h[at, :], u_l[at, :] = split(u - mul((high[:, half:], low[:, half:]), ct))

        def powers(left, right, bound):
            first = (eye + mul(left, right)) * (1.0 / (1.0 + bound))
            pieces = split(first)
            second = mul(pieces, pieces)
            return first, second, mul(split(second), pieces)

        kept_powers = powers(c, ct, own)
        c = split(behind)
        ct = split(behind.T)
        own_behind = total(behind * behind)
        moved_powers = powers(ct, c, own_behind)

        others = pl.ds(0, column - 1)
        wait(peaks.at[t, others], peak_recv.at[t])

        @pl.when(jnp.logical_not(last_z))
        def _():
            for k, (start, size) in enumerate(PIECES):
                at = pl.ds(start, size)
                send(v_out.at[t, at], v_in.at[t, at], v_send.at[t, k], v_recv.at[t, k], following)

        def forward(k):
            at = pl.ds(*PIECES[k])
            wait(pass_in.at[t, at], pass_recv.at[t, k])
            send(pass_in.at[t, at], v_in.at[t, at], v_send.at[t, k], v_recv.at[t, k], next_z)

        @pl.when(last_z)
        def _():
            for k in range(EARLY):
                forward(k)

        largest = jnp.max(peaks[t], axis=0)[0:1, 0:1]
        root = lax.rsqrt(1.0 + largest)
        factors = []
        for (first, second, third), bound in ((kept_powers, own), (moved_powers, own_behind)):
            ratio = (1.0 + bound) / (1.0 + largest)
            n1 = (2.25 * ratio) * first - (1.5 * ratio * ratio) * second
            n1 = n1 + (0.25 * ratio * ratio * ratio) * third
            t1 = split(1.5 * eye - 0.5 * n1)
            q1 = root * (1.5 * eye - (0.5 * ratio) * first)
            n2 = mul(split(mul(split(n1), t1)), t1)
            q2 = mul(split(q1), t1)
            t2 = split(1.5 * eye - 0.5 * n2)
            factors.append(split(mul(split(q2), t2)))

        @pl.when(last_z)
        def _():
            for k in range(EARLY, len(PIECES)):
                forward(k)

    for chunk in range(CHUNKS):
        at = pl.ds(chunk * step, step)
        out_ref[at, :] = finished(n_rounds - 1, chunk)

    for t in range(n_rounds):
        wait(gram_out.at[t, seven], gram_send.at[t])
        wait(parts.at[t, all_but_one], part_send.at[t])
        wait(slices.at[t, seven], slice_send.at[t])
        wait(peaks.at[t, others], peak_send.at[t])
        wait(behinds.at[t], c_send.at[t])
        for k, (start, size) in enumerate(RAW):
            wait(raw_out.at[t, pl.ds(start, size)], raw_send.at[t, k])
        for k, (start, size) in enumerate(PIECES):
            wait(v_out.at[t, pl.ds(start, size)], v_send.at[t, k])

        @pl.when(last_z)
        def _():
            wait(crosses.at[t], d_send.at[t])
            for k, (start, size) in enumerate(PIECES):
                wait(v_out.at[t, pl.ds(start, size)], pass_send.at[t, k])

        @pl.when(first_z)
        def _():
            for k, (start, size) in enumerate(RELAY):
                wait(v_out.at[t, pl.ds(start, size)], relay_send.at[t, k])


def solution(mesh):
    n_wide, n_rows = mesh.shape["wide"], mesh.shape["rows"]

    def shards(matrix, pairing):
        rows, width = matrix.shape
        half = width // 2
        part = half // n_rows
        n_rounds = pairing.shape[0]
        raw_rows = sum(size for _, size in RAW)
        hbm = pl.BlockSpec(memory_space=pltpu.HBM)
        dma = pltpu.SemaphoreType.DMA

        def f32(*shape):
            return pltpu.VMEM(shape, F32)

        def bf16(*shape):
            return pltpu.VMEM(shape, BF16)

        return pl.pallas_call(
            functools.partial(kernel, n_wide, n_rows, n_rounds),
            out_shape=jax.ShapeDtypeStruct(matrix.shape, F32),
            in_specs=[hbm, hbm],
            out_specs=pl.BlockSpec(memory_space=pltpu.VMEM),
            scratch_shapes=[
                f32(rows, width),
                pltpu.VMEM(pairing.shape, pairing.dtype),
                f32(n_rounds, n_rows, part + 8, half),
                f32(n_rounds, n_rows, part + 8, half),
                f32(n_rounds, 8, 128),
                f32(n_rounds, 2 * n_rows, 8, 128),
                f32(n_rounds, part, half),
                f32(n_rounds, n_rows, part, half),
                f32(n_rounds, 8, 128),
                f32(n_rounds, n_wide // 2, 8, 128),
                f32(n_rounds, raw_rows, width),
                f32(n_rounds, raw_rows, width),
                f32(n_rounds, rows, half),
                f32(n_rounds, rows, half),
                f32(n_rounds, n_rows, part, half),
                f32(n_rounds, n_rows, part, half),
                f32(half, half),
                f32(n_rounds, rows, half),
                bf16(rows, width), bf16(rows, width),
                bf16(rows, half), bf16(rows, half), bf16(rows, half), bf16(rows, half),
                f32(half, half),
                f32(1, width),
                dma((CHUNKS,)), dma,
                dma((n_rounds,)), dma((n_rounds,)), dma((n_rounds,)), dma((n_rounds,)),
                dma((n_rounds,)), dma((n_rounds,)), dma((n_rounds,)), dma((n_rounds,)),
                dma((n_rounds, len(RAW))), dma((n_rounds, len(RAW))),
                dma((n_rounds, len(PIECES))), dma((n_rounds, len(PIECES))),
                dma((n_rounds, len(RELAY))), dma((n_rounds, len(RELAY))),
                dma((n_rounds, len(PIECES))), dma((n_rounds, len(PIECES))),
                dma((n_rounds,)), dma((n_rounds,)), dma((n_rounds,)), dma((n_rounds,)),
            ],
            compiler_params=pltpu.CompilerParams(
                collective_id=0, has_side_effects=True, vmem_limit_bytes=48 * 1024 * 1024
            ),
        )(matrix, pairing)

    return jax.shard_map(
        shards, mesh=mesh, in_specs=(P("rows", "wide"), P()), out_specs=P("rows", "wide"),
        check_vma=False,
    )
```
